32 devices in a mesh: src: 8 (over y, x, core), dst: 4 (over z).
Axes of the slice: x: 2, y: 2, z: 4, core: 2. Of those that a mesh axis runs over, the one named last changes fastest.
Arguments:
- raw: bfloat16 [4096, 256], P(('src', 'dst')), may hold values from -6 to 6
- enc_w1: bfloat16 [256, 512], replicated, may hold values from -0.375 to 0.375
- enc_w2: bfloat16 [512, 256], replicated, may hold values from -0.25 to 0.25
- block_weights: float32 [512, 128, 128], P(('src', 'dst')), may hold values from -0.125 to 0.125
- block_cols: int32 [512], P(('src', 'dst')), may hold values from 0 to 3, as said below
- noise: bfloat16 [3, 4096, 256], P(None, ('src', 'dst')), may hold values from -3 to 3
Outputs:
- encoded: bfloat16 [4096, 256], P(('src', 'dst'))
- hops: bfloat16 [3, 4096, 256], P(None, ('src', 'dst'))
The draws below stay inside these ranges and needn't reach their ends.
Inputs may be any that keep to these rules, and one draw needn't show every extreme that they name: `block_cols`: entry b of each device's 16 entries belongs to row block b // 2; row blocks 2j and 2j+1 of a device together name every column block exactly once, each naming 4 // 2 distinct ones.
All inputs are finite; a program needn't handle non-finite values.
Results may differ from the reference program's by a relative error of at most 0.0058.
Values may be sent and summed in bfloat16 or wider, within the bound.
A program may use at most 128 MiB of HBM per device.

```python
import jax
import jax.numpy as jnp
from jax import lax

F_IN = 256
HID = 512
W = 256
BS = 128
HOPS = 3
ROWS_DEV = 128
NODES = 4096
GR = 8
GC = 4
BLK_DEV = 16
BLOCKS = 512
N_SRC = 8
N_DST = 4


def draw_block_cols(key, part):
    pairs = N_SRC * N_DST * (GR // 2)
    keys = jax.random.split(jax.random.fold_in(key, 7), pairs)
    perms = jax.vmap(lambda sub: jax.random.permutation(sub, GC))(keys)
    return perms.reshape(BLOCKS).astype(jnp.int32)


def block_scale(rng, dims, pieces, smallest, largest):
    def one(position, blocks):
        draws = jax.random.uniform(jax.random.fold_in(jax.random.fold_in(rng, 6), position), (blocks,), jnp.float32, smallest / len(pieces), largest / len(pieces))
        return jnp.repeat(jnp.exp(draws), dims[position] // blocks).reshape((-1,) + (1,) * (len(dims) - position - 1))

    gain = one(*pieces[0])
    for cut in pieces[1:]:
        gain = gain * one(*cut)
    return gain


def centred(key, dims, deviation, limit, cuts=(), kind=jnp.bfloat16):
    result = deviation * jax.random.normal(key, dims, jnp.float32)
    if cuts:
        result = result * block_scale(key, dims, cuts, -0.22, 0.18)
    return jnp.clip(result, -limit, limit).astype(kind)


def setup_inputs(seed: int = 0) -> dict:
    key_list = jax.random.split(jax.random.key(seed), 7)
    raw = centred(key_list[0], (NODES, F_IN), 1.0, 6.0, ((0, 32),))
    enc_w1 = centred(key_list[1], (F_IN, HID), F_IN ** -0.5, 0.375)
    enc_w2 = centred(key_list[2], (HID, W), HID ** -0.5, 0.25)
    block_weights = centred(key_list[3], (BLOCKS, BS, BS), (N_SRC * N_DST * ROWS_DEV // 2) ** -0.5, 0.125, ((0, 32),), jnp.float32)
    block_cols = draw_block_cols(jax.random.fold_in(key_list[6], 71), 0)
    noise = centred(key_list[5], (HOPS, NODES, W), 0.5, 3.0, ((1, 32),))
    return {"raw": raw, "enc_w1": enc_w1, "enc_w2": enc_w2, "block_weights": block_weights, "block_cols": block_cols, "noise": noise}


def normalize_rows(z):
    return (z * lax.rsqrt(lax.optimization_barrier(jnp.mean(z * z, axis=-1, keepdims=True)) + 1e-06)).astype(jnp.bfloat16)

def reference(raw, enc_w1, enc_w2, block_weights, block_cols, noise):
    hidden = jax.nn.silu(jnp.dot(raw, enc_w1, preferred_element_type=jnp.float32)).astype(jnp.bfloat16)
    encoded = normalize_rows(jnp.dot(hidden, enc_w2, preferred_element_type=jnp.float32))
    weights = block_weights.reshape(N_SRC, N_DST, BLK_DEV, BS, BS)
    columns = block_cols.reshape(N_SRC, N_DST, BLK_DEV)
    half = GC // 2
    feats = encoded
    kept = []
    for step in range(HOPS):
        col_blocks = feats.astype(jnp.float32).reshape(N_SRC, GC, BS, W)

        def one_dest(dest):
            w_dest = lax.dynamic_index_in_dim(weights, dest, 1, keepdims=False)
            c_dest = lax.dynamic_index_in_dim(columns, dest, 1, keepdims=False)
            fetched = jax.vmap(lambda blocks, cols: jnp.take(blocks, cols, axis=0))(col_blocks, c_dest)
            prods = jnp.einsum('sbij,sbjw->sbiw', w_dest, fetched, precision=lax.Precision.HIGHEST)
            return prods.reshape(N_SRC, GR, half, BS, W).sum(axis=(0, 2)).reshape(N_SRC, ROWS_DEV, W)
        agg = lax.map(one_dest, jnp.arange(N_DST, dtype=jnp.int32))
        agg = jnp.transpose(agg, (1, 0, 2, 3)).reshape(NODES, W)
        feats = normalize_rows(agg + noise[step].astype(jnp.float32))
        kept.append(feats)
    return (encoded, jnp.stack(kept))
```

```python
import functools

import jax
import jax.numpy as jnp
from jax import lax
from jax.experimental import pallas as pl
from jax.experimental.pallas import tpu as pltpu
from jax.sharding import PartitionSpec as P

MESH = pl.DeviceIdType.MESH
CHUNKS = 2
F32 = jnp.float32
BF16 = jnp.bfloat16


def shifted(me, step, count):
    if count & (count - 1) == 0:
        return me ^ step, me ^ step
    return lax.rem(me + step, count), lax.rem(me + count - step, count)


def kernel(
    n_src, n_dst, hops,
    raw_h, w1_h, w2_h, bw_h, cols, noise_h,
    enc_h, hops_h,
    raw_v, w1_v, w2_v, bw_v, noise_v, enc_v, hops_v, wcat, gath, out1, in1, out2, in2, acc,
    load_sem, store_sem, g_send, g_recv, send1, recv1, send2, recv2,
):
    src, dst = lax.axis_index("src"), lax.axis_index("dst")
    pairs = n_src // 2
    pair, core = src // 2, lax.rem(src, 2)
    partner = pair * 2 + 1 - core
    side = bw_v.shape[1]
    per_row = bw_v.shape[0] // n_src
    width = enc_v.shape[1]
    part = width // CHUNKS

    loads = [
        pltpu.make_async_copy(a, b, load_sem.at[i])
        for i, (a, b) in enumerate(
            ((raw_h, raw_v), (w1_h, w1_v), (w2_h, w2_v), (bw_h, bw_v), (noise_h, noise_v))
        )
    ]
    for load in loads:
        load.start()

    barrier = pltpu.get_barrier_semaphore()
    greeted = 0
    for step in range(1, n_dst):
        to, _ = shifted(dst, step, n_dst)
        pl.semaphore_signal(barrier, inc=1, device_id={"dst": to}, device_id_type=MESH)
        greeted += 1
    for step in range(1, pairs):
        to, _ = shifted(pair, step, pairs)
        pl.semaphore_signal(barrier, inc=1, device_id={"src": to * 2 + core}, device_id_type=MESH)
        greeted += 1
    pl.semaphore_signal(barrier, inc=1, device_id={"src": partner}, device_id_type=MESH)
    greeted += 1

    def normalized(z):
        scale = lax.rsqrt(jnp.sum(z * z, axis=-1, keepdims=True) * (1.0 / width) + 1e-06)
        return (z * scale).astype(BF16)

    loads[0].wait()
    loads[1].wait()
    v = jnp.dot(raw_v[...], w1_v[...], preferred_element_type=F32)
    hidden = (v * jax.nn.sigmoid(v)).astype(BF16)
    loads[2].wait()
    feats = normalized(jnp.dot(hidden, w2_v[...], preferred_element_type=F32))
    enc_v[...] = feats
    stores = [pltpu.make_async_copy(enc_v, enc_h, store_sem.at[0])]
    stores[0].start()

    pl.semaphore_wait(barrier, greeted)
    sent = []

    def gather(hop, feats):
        waits = []
        for c in range(CHUNKS):
            gath[hop][c][dst] = feats[:, c * part : (c + 1) * part]
        for c in range(CHUNKS):
            buf = gath[hop][c]
            mine = []
            for step in reversed(range(1, n_dst)):
                to, _ = shifted(dst, step, n_dst)
                copy = pltpu.make_async_remote_copy(
                    src_ref=buf.at[dst],
                    dst_ref=buf.at[dst],
                    send_sem=g_send.at[hop, c, step - 1],
                    recv_sem=g_recv.at[hop, c, step - 1],
                    device_id={"dst": to},
                    device_id_type=MESH,
                )
                copy.start()
                mine.append(copy)
            waits.append(mine)
            sent.extend(mine)
        return waits

    waits = gather(0, feats)

    loads[3].wait()
    for b in range(bw_v.shape[0]):
        r, i = divmod(b, per_row)
        w = bw_v[b]
        high = w.astype(BF16)
        wcat[r, 0:side, i * side : (i + 1) * side] = high
        wcat[r, side : 2 * side, i * side : (i + 1) * side] = (w - high.astype(F32)).astype(BF16)
    loads[4].wait()

    order = list(reversed(range(pairs)))
    for hop in range(hops):
        arrivals = []
        for c in range(CHUNKS):
            buf = gath[hop][c]
            for copy in waits[c]:
                copy.wait_recv()

            def product(row):
                picked = [buf[cols[row * per_row + i]] for i in range(per_row)]
                both = jnp.dot(
                    wcat[row], jnp.concatenate(picked, axis=0), preferred_element_type=F32
                )
                return both[:side] + both[side:]

            first = {}
            for step in order:
                to, _ = shifted(pair, step, pairs) if step else (pair, pair)
                out1[hop, c, step] = product(to * 2 + 1 - core).astype(BF16)
                copy = pltpu.make_async_remote_copy(
                    src_ref=out1.at[hop, c, step],
                    dst_ref=in1.at[hop, c, step],
                    send_sem=send1.at[hop, c, step],
                    recv_sem=recv1.at[hop, c, step],
                    device_id={"src": partner},
                    device_id_type=MESH,
                )
                copy.start()
                first[step] = copy
                sent.append(copy)
            second = []
            for step in order:
                to, _ = shifted(pair, step, pairs) if step else (pair, pair)
                mine = product(to * 2 + core)
                first[step].wait_recv()
                mine = mine + in1[hop, c, step].astype(F32)
                if step == 0:
                    acc[c] = mine
                    continue
                out2[hop, c, step - 1] = mine.astype(BF16)
                copy = pltpu.make_async_remote_copy(
                    src_ref=out2.at[hop, c, step - 1],
                    dst_ref=in2.at[hop, c, step - 1],
                    send_sem=send2.at[hop, c, step - 1],
                    recv_sem=recv2.at[hop, c, step - 1],
                    device_id={"src": to * 2 + core},
                    device_id_type=MESH,
                )
                copy.start()
                second.append(copy)
                sent.append(copy)
            arrivals.append(second)
        sums = []
        for c in range(CHUNKS):
            z = acc[c] + noise_v[hop, :, c * part : (c + 1) * part].astype(F32)
            for copy in arrivals[c]:
                copy.wait_recv()
            for step in range(1, pairs):
                z = z + in2[hop, c, step - 1].astype(F32)
            sums.append(z)
        feats = normalized(jnp.concatenate(sums, axis=1) if CHUNKS > 1 else sums[0])
        if hop < hops - 1:
            waits = gather(hop + 1, feats)
        hops_v[hop] = feats
        store = pltpu.make_async_copy(hops_v.at[hop], hops_h.at[hop], store_sem.at[hop + 1])
        store.start()
        stores.append(store)
    for copy in sent:
        copy.wait_send()
    for store in stores:
        store.wait()


def shards(n_src, n_dst, raw, enc_w1, enc_w2, block_weights, block_cols, noise):
    blocks, side, _ = block_weights.shape
    hops, rows, width = noise.shape
    pairs = n_src // 2
    per_row = blocks // n_src
    part = width // CHUNKS
    assert rows == side and n_src % 2 == 0
    anywhere = pl.BlockSpec(memory_space=pl.ANY)
    dma = pltpu.SemaphoreType.DMA
    far = max(pairs - 1, 1)
    near = max(n_dst - 1, 1)
    return pl.pallas_call(
        functools.partial(kernel, n_src, n_dst, hops),
        out_shape=(
            jax.ShapeDtypeStruct((rows, width), BF16),
            jax.ShapeDtypeStruct((hops, rows, width), BF16),
        ),
        in_specs=[anywhere] * 4 + [pl.BlockSpec(memory_space=pltpu.SMEM), anywhere],
        out_specs=(anywhere, anywhere),
        scratch_shapes=[
            pltpu.VMEM(raw.shape, BF16),
            pltpu.VMEM(enc_w1.shape, BF16),
            pltpu.VMEM(enc_w2.shape, BF16),
            pltpu.VMEM(block_weights.shape, F32),
            pltpu.VMEM(noise.shape, BF16),
            pltpu.VMEM((rows, width), BF16),
            pltpu.VMEM((hops, rows, width), BF16),
            pltpu.VMEM((n_src, 2 * side, per_row * side), BF16),
            [[pltpu.VMEM((n_dst, rows, part), BF16) for _ in range(CHUNKS)] for _ in range(hops)],
            pltpu.VMEM((hops, CHUNKS, pairs, rows, part), BF16),
            pltpu.VMEM((hops, CHUNKS, pairs, rows, part), BF16),
            pltpu.VMEM((hops, CHUNKS, far, rows, part), BF16),
            pltpu.VMEM((hops, CHUNKS, far, rows, part), BF16),
            pltpu.VMEM((CHUNKS, rows, part), F32),
            dma((5,)),
            dma((hops + 1,)),
            dma((hops, CHUNKS, near)),
            dma((hops, CHUNKS, near)),
            dma((hops, CHUNKS, pairs)),
            dma((hops, CHUNKS, pairs)),
            dma((hops, CHUNKS, far)),
            dma((hops, CHUNKS, far)),
        ],
        compiler_params=pltpu.CompilerParams(
            collective_id=0, has_side_effects=True, vmem_limit_bytes=60 * 1024 * 1024
        ),
    )(raw, enc_w1, enc_w2, block_weights, block_cols, noise)


def solution(mesh):
    placed = (
        P(("src", "dst"), None),
        P(),
        P(),
        P(("src", "dst"), None, None),
        P(("src", "dst")),
        P(None, ("src", "dst"), None),
    )
    return jax.shard_map(
        functools.partial(shards, mesh.shape["src"], mesh.shape["dst"]),
        mesh=mesh,
        in_specs=placed,
        out_specs=(P(("src", "dst"), None), P(None, ("src", "dst"), None)),
        check_vma=False,
    )
```

```python
import functools

import jax
import jax.numpy as jnp
from jax import lax
from jax.experimental import pallas as pl
from jax.experimental.pallas import tpu as pltpu
from jax.sharding import PartitionSpec as P

MESH = pl.DeviceIdType.MESH
CHUNKS = 2
F32 = jnp.float32
BF16 = jnp.bfloat16


def shifted(me, step, count):
    if count & (count - 1) == 0:
        return me ^ step, me ^ step
    return lax.rem(me + step, count), lax.rem(me + count - step, count)


def kernel(
    n_src, n_dst, hops,
    raw_h, w1_h, w2_h, bw_h, cols, noise_h,
    enc_h, hops_h,
    raw_v, w1_v, w2_v, bw_v, noise_v, enc_v, hops_v, wcat, gath, out1, in1, out2, in2, acc,
    load_sem, store_sem, g_send, g_recv, send1, recv1, send2, recv2,
):
    src, dst = lax.axis_index("src"), lax.axis_index("dst")
    pairs = n_src // 2
    pair, core = src // 2, lax.rem(src, 2)
    partner = pair * 2 + 1 - core
    side = bw_v.shape[1]
    per_row = bw_v.shape[0] // n_src
    width = enc_v.shape[1]
    part = width // CHUNKS

    barrier = pltpu.get_barrier_semaphore()
    greeted = 0
    for step in range(1, n_dst):
        to, _ = shifted(dst, step, n_dst)
        pl.semaphore_signal(barrier, inc=1, device_id={"dst": to}, device_id_type=MESH)
        greeted += 1
    for step in range(1, pairs):
        to, _ = shifted(pair, step, pairs)
        pl.semaphore_signal(barrier, inc=1, device_id={"src": to * 2 + core}, device_id_type=MESH)
        greeted += 1
    pl.semaphore_signal(barrier, inc=1, device_id={"src": partner}, device_id_type=MESH)
    greeted += 1

    loads = [
        pltpu.make_async_copy(a, b, load_sem.at[i])
        for i, (a, b) in enumerate(
            ((raw_h, raw_v), (w1_h, w1_v), (w2_h, w2_v), (bw_h, bw_v), (noise_h, noise_v))
        )
    ]
    for load in loads:
        load.start()

    def normalized(z):
        scale = lax.rsqrt(jnp.sum(z * z, axis=-1, keepdims=True) * (1.0 / width) + 1e-06)
        return (z * scale).astype(BF16)

    loads[0].wait()
    loads[1].wait()
    v = jnp.dot(raw_v[...], w1_v[...], preferred_element_type=F32)
    hidden = (v * jax.nn.sigmoid(v)).astype(BF16)
    loads[2].wait()
    feats = normalized(jnp.dot(hidden, w2_v[...], preferred_element_type=F32))
    enc_v[...] = feats
    stores = [pltpu.make_async_copy(enc_v, enc_h, store_sem.at[0])]
    stores[0].start()

    pl.semaphore_wait(barrier, greeted)
    sent = []

    def gather(hop, feats):
        waits = []
        for c in range(CHUNKS):
            gath[hop][c][dst] = feats[:, c * part : (c + 1) * part]
        for c in range(CHUNKS):
            buf = gath[hop][c]
            mine = []
            for step in range(1, n_dst):
                to, _ = shifted(dst, step, n_dst)
                copy = pltpu.make_async_remote_copy(
                    src_ref=buf.at[dst],
                    dst_ref=buf.at[dst],
                    send_sem=g_send.at[hop, c, step - 1],
                    recv_sem=g_recv.at[hop, c, step - 1],
                    device_id={"dst": to},
                    device_id_type=MESH,
                )
                copy.start()
                mine.append(copy)
            waits.append(mine)
            sent.extend(mine)
        return waits

    waits = gather(0, feats)

    loads[3].wait()
    for b in range(bw_v.shape[0]):
        r, i = divmod(b, per_row)
        w = bw_v[b]
        high = w.astype(BF16)
        wcat[r, 0:side, i * side : (i + 1) * side] = high
        wcat[r, side : 2 * side, i * side : (i + 1) * side] = (w - high.astype(F32)).astype(BF16)
    loads[4].wait()

    order = list(reversed(range(pairs)))
    for hop in range(hops):
        arrivals = []
        for c in range(CHUNKS):
            buf = gath[hop][c]
            for copy in waits[c]:
                copy.wait_recv()

            def product(row):
                picked = [buf[cols[row * per_row + i]] for i in range(per_row)]
                both = jnp.dot(
                    wcat[row], jnp.concatenate(picked, axis=0), preferred_element_type=F32
                )
                return both[:side] + both[side:]

            first = {}
            for step in order:
                to, _ = shifted(pair, step, pairs) if step else (pair, pair)
                out1[hop, c, step] = product(to * 2 + 1 - core).astype(BF16)
                copy = pltpu.make_async_remote_copy(
                    src_ref=out1.at[hop, c, step],
                    dst_ref=in1.at[hop, c, step],
                    send_sem=send1.at[hop, c, step],
                    recv_sem=recv1.at[hop, c, step],
                    device_id={"src": partner},
                    device_id_type=MESH,
                )
                copy.start()
                first[step] = copy
                sent.append(copy)
            second = []
            for step in order:
                to, _ = shifted(pair, step, pairs) if step else (pair, pair)
                mine = product(to * 2 + core)
                first[step].wait_recv()
                mine = mine + in1[hop, c, step].astype(F32)
                if step == 0:
                    acc[c] = mine
                    continue
                out2[hop, c, step - 1] = mine.astype(BF16)
                copy = pltpu.make_async_remote_copy(
                    src_ref=out2.at[hop, c, step - 1],
                    dst_ref=in2.at[hop, c, step - 1],
                    send_sem=send2.at[hop, c, step - 1],
                    recv_sem=recv2.at[hop, c, step - 1],
                    device_id={"src": to * 2 + core},
                    device_id_type=MESH,
                )
                copy.start()
                second.append(copy)
                sent.append(copy)
            arrivals.append(second)
        sums = []
        for c in range(CHUNKS):
            z = acc[c] + noise_v[hop, :, c * part : (c + 1) * part].astype(F32)
            for copy in arrivals[c]:
                copy.wait_recv()
            for step in range(1, pairs):
                z = z + in2[hop, c, step - 1].astype(F32)
            sums.append(z)
        feats = normalized(jnp.concatenate(sums, axis=1) if CHUNKS > 1 else sums[0])
        if hop < hops - 1:
            waits = gather(hop + 1, feats)
        hops_v[hop] = feats
        store = pltpu.make_async_copy(hops_v.at[hop], hops_h.at[hop], store_sem.at[hop + 1])
        store.start()
        stores.append(store)
    for copy in sent:
        copy.wait_send()
    for store in stores:
        store.wait()


def finish(enc_i, hops_i, enc_o, hops_o, enc_v, hops_v, sem):
    reads = [
        pltpu.make_async_copy(hops_i, hops_v, sem.at[0]),
        pltpu.make_async_copy(enc_i, enc_v, sem.at[1]),
    ]
    writes = [
        pltpu.make_async_copy(hops_v, hops_o, sem.at[2]),
        pltpu.make_async_copy(enc_v, enc_o, sem.at[3]),
    ]
    for read in reads:
        read.start()
    for read, write in zip(reads, writes):
        read.wait()
        write.start()
    for write in writes:
        write.wait()


def shards(n_src, n_dst, raw, enc_w1, enc_w2, block_weights, block_cols, noise):
    blocks, side, _ = block_weights.shape
    hops, rows, width = noise.shape
    pairs = n_src // 2
    per_row = blocks // n_src
    part = width // CHUNKS
    assert rows == side and n_src % 2 == 0
    anywhere = pl.BlockSpec(memory_space=pl.ANY)
    dma = pltpu.SemaphoreType.DMA
    far = max(pairs - 1, 1)
    near = max(n_dst - 1, 1)
    encoded, kept = pl.pallas_call(
        functools.partial(kernel, n_src, n_dst, hops),
        out_shape=(
            jax.ShapeDtypeStruct((rows, width), BF16),
            jax.ShapeDtypeStruct((hops, rows, width), BF16),
        ),
        in_specs=[anywhere] * 4 + [pl.BlockSpec(memory_space=pltpu.SMEM), anywhere],
        out_specs=(anywhere, anywhere),
        scratch_shapes=[
            pltpu.VMEM(raw.shape, BF16),
            pltpu.VMEM(enc_w1.shape, BF16),
            pltpu.VMEM(enc_w2.shape, BF16),
            pltpu.VMEM(block_weights.shape, F32),
            pltpu.VMEM(noise.shape, BF16),
            pltpu.VMEM((rows, width), BF16),
            pltpu.VMEM((hops, rows, width), BF16),
            pltpu.VMEM((n_src, 2 * side, per_row * side), BF16),
            [[pltpu.VMEM((n_dst, rows, part), BF16) for _ in range(CHUNKS)] for _ in range(hops)],
            pltpu.VMEM((hops, CHUNKS, pairs, rows, part), BF16),
            pltpu.VMEM((hops, CHUNKS, pairs, rows, part), BF16),
            pltpu.VMEM((hops, CHUNKS, far, rows, part), BF16),
            pltpu.VMEM((hops, CHUNKS, far, rows, part), BF16),
            pltpu.VMEM((CHUNKS, rows, part), F32),
            dma((5,)),
            dma((hops + 1,)),
            dma((hops, CHUNKS, near)),
            dma((hops, CHUNKS, near)),
            dma((hops, CHUNKS, pairs)),
            dma((hops, CHUNKS, pairs)),
            dma((hops, CHUNKS, far)),
            dma((hops, CHUNKS, far)),
        ],
        compiler_params=pltpu.CompilerParams(
            collective_id=0, has_side_effects=True, vmem_limit_bytes=60 * 1024 * 1024
        ),
    )(raw, enc_w1, enc_w2, block_weights, block_cols, noise)
    shapes = (
        jax.ShapeDtypeStruct((rows, width), BF16),
        jax.ShapeDtypeStruct((hops, rows, width), BF16),
    )
    return pl.pallas_call(
        finish,
        out_shape=shapes,
        in_specs=[anywhere, anywhere],
        out_specs=(anywhere, anywhere),
        scratch_shapes=[pltpu.VMEM(s.shape, BF16) for s in shapes] + [dma((4,))],
    )(encoded, kept)


def solution(mesh):
    placed = (
        P(("src", "dst"), None),
        P(),
        P(),
        P(("src", "dst"), None, None),
        P(("src", "dst")),
        P(None, ("src", "dst"), None),
    )
    return jax.shard_map(
        functools.partial(shards, mesh.shape["src"], mesh.shape["dst"]),
        mesh=mesh,
        in_specs=placed,
        out_specs=(P(("src", "dst"), None), P(None, ("src", "dst"), None)),
        check_vma=False,
    )
```

```python
import functools

import jax
import jax.numpy as jnp
from jax import lax
from jax.experimental import pallas as pl
from jax.experimental.pallas import tpu as pltpu
from jax.sharding import PartitionSpec as P

MESH = pl.DeviceIdType.MESH
CHUNKS = 2
F32 = jnp.float32
BF16 = jnp.bfloat16


def shifted(me, step, count):
    if count & (count - 1) == 0:
        return me ^ step, me ^ step
    return lax.rem(me + step, count), lax.rem(me + count - step, count)


def kernel(
    n_src, n_dst, hops,
    raw_h, w1_h, w2_h, bw_h, cols, noise_h,
    enc_h, hops_h,
    raw_v, w1_v, w2_v, bw_v, noise_v, enc_v, hops_v, wcat, gath, out1, in1, out2, in2, acc,
    load_sem, store_sem, g_send, g_recv, send1, recv1, send2, recv2,
):
    src, dst = lax.axis_index("src"), lax.axis_index("dst")
    pairs = n_src // 2
    pair, core = src // 2, lax.rem(src, 2)
    partner = pair * 2 + 1 - core
    side = bw_v.shape[1]
    per_row = bw_v.shape[0] // n_src
    width = enc_v.shape[1]
    part = width // CHUNKS

    barrier = pltpu.get_barrier_semaphore()
    greeted = 0
    for step in range(1, n_dst):
        to, _ = shifted(dst, step, n_dst)
        pl.semaphore_signal(barrier, inc=1, device_id={"dst": to}, device_id_type=MESH)
        greeted += 1
    for step in range(1, pairs):
        to, _ = shifted(pair, step, pairs)
        pl.semaphore_signal(barrier, inc=1, device_id={"src": to * 2 + core}, device_id_type=MESH)
        greeted += 1
    pl.semaphore_signal(barrier, inc=1, device_id={"src": partner}, device_id_type=MESH)
    greeted += 1

    loads = [
        pltpu.make_async_copy(a, b, load_sem.at[i])
        for i, (a, b) in enumerate(
            ((raw_h, raw_v), (w1_h, w1_v), (w2_h, w2_v), (bw_h, bw_v), (noise_h, noise_v))
        )
    ]
    for load in loads:
        load.start()

    def normalized(z):
        scale = lax.rsqrt(jnp.sum(z * z, axis=-1, keepdims=True) * (1.0 / width) + 1e-06)
        return (z * scale).astype(BF16)

    loads[0].wait()
    loads[1].wait()
    v = jnp.dot(raw_v[...], w1_v[...], preferred_element_type=F32)
    hidden = (v * jax.nn.sigmoid(v)).astype(BF16)
    loads[2].wait()
    feats = normalized(jnp.dot(hidden, w2_v[...], preferred_element_type=F32))
    enc_v[...] = feats
    stores = [pltpu.make_async_copy(enc_v, enc_h, store_sem.at[0])]
    stores[0].start()

    pl.semaphore_wait(barrier, greeted)
    sent = []

    def gather(hop, feats):
        waits = []
        for c in range(CHUNKS):
            gath[hop][c][dst] = feats[:, c * part : (c + 1) * part]
        for c in range(CHUNKS):
            buf = gath[hop][c]
            mine = []
            for step in range(1, n_dst):
                to, _ = shifted(dst, step, n_dst)
                copy = pltpu.make_async_remote_copy(
                    src_ref=buf.at[dst],
                    dst_ref=buf.at[dst],
                    send_sem=g_send.at[hop, c, step - 1],
                    recv_sem=g_recv.at[hop, c, step - 1],
                    device_id={"dst": to},
                    device_id_type=MESH,
                )
                copy.start()
                mine.append(copy)
            waits.append(mine)
            sent.extend(mine)
        return waits

    waits = gather(0, feats)

    loads[3].wait()
    for b in range(bw_v.shape[0]):
        r, i = divmod(b, per_row)
        w = bw_v[b]
        high = w.astype(BF16)
        wcat[r, 0:side, i * side : (i + 1) * side] = high
        wcat[r, side : 2 * side, i * side : (i + 1) * side] = (w - high.astype(F32)).astype(BF16)
    loads[4].wait()

    order = list(reversed(range(pairs)))
    def at(step):
        return shifted(pair, step, pairs)[0] if step else pair

    named = {
        (step, side_core): [
            cols[(at(step) * 2 + (core if side_core else 1 - core)) * per_row + i]
            for i in range(per_row)
        ]
        for step in order
        for side_core in (0, 1)
    }
    for hop in range(hops):
        arrivals = []
        for c in range(CHUNKS):
            buf = gath[hop][c]
            for copy in waits[c]:
                copy.wait_recv()

            def product(row, step, own):
                picked = [buf[name] for name in named[step, own]]
                both = jnp.dot(
                    wcat[row], jnp.concatenate(picked, axis=0), preferred_element_type=F32
                )
                return both[:side] + both[side:]

            first = {}
            for step in order:
                to, _ = shifted(pair, step, pairs) if step else (pair, pair)
                out1[hop, c, step] = product(to * 2 + 1 - core, step, 0).astype(BF16)
                copy = pltpu.make_async_remote_copy(
                    src_ref=out1.at[hop, c, step],
                    dst_ref=in1.at[hop, c, step],
                    send_sem=send1.at[hop, c, step],
                    recv_sem=recv1.at[hop, c, step],
                    device_id={"src": partner},
                    device_id_type=MESH,
                )
                copy.start()
                first[step] = copy
                sent.append(copy)
            second = []
            for step in order:
                to, _ = shifted(pair, step, pairs) if step else (pair, pair)
                mine = product(to * 2 + core, step, 1)
                first[step].wait_recv()
                mine = mine + in1[hop, c, step].astype(F32)
                if step == 0:
                    acc[c] = mine
                    continue
                out2[hop, c, step - 1] = mine.astype(BF16)
                copy = pltpu.make_async_remote_copy(
                    src_ref=out2.at[hop, c, step - 1],
                    dst_ref=in2.at[hop, c, step - 1],
                    send_sem=send2.at[hop, c, step - 1],
                    recv_sem=recv2.at[hop, c, step - 1],
                    device_id={"src": to * 2 + core},
                    device_id_type=MESH,
                )
                copy.start()
                second.append(copy)
                sent.append(copy)
            arrivals.append(second)
        sums = []
        for c in range(CHUNKS):
            z = acc[c] + noise_v[hop, :, c * part : (c + 1) * part].astype(F32)
            for step in range(1, pairs):
                arrivals[c][pairs - 1 - step].wait_recv()
                z = z + in2[hop, c, step - 1].astype(F32)
            sums.append(z)
        feats = normalized(jnp.concatenate(sums, axis=1) if CHUNKS > 1 else sums[0])
        if hop < hops - 1:
            waits = gather(hop + 1, feats)
        hops_v[hop] = feats
        store = pltpu.make_async_copy(hops_v.at[hop], hops_h.at[hop], store_sem.at[hop + 1])
        store.start()
        stores.append(store)
    for copy in sent:
        copy.wait_send()
    for store in stores:
        store.wait()


def finish(enc_i, hops_i, enc_o, hops_o, enc_v, hops_v, sem):
    reads = [
        pltpu.make_async_copy(hops_i, hops_v, sem.at[0]),
        pltpu.make_async_copy(enc_i, enc_v, sem.at[1]),
    ]
    writes = [
        pltpu.make_async_copy(hops_v, hops_o, sem.at[2]),
        pltpu.make_async_copy(enc_v, enc_o, sem.at[3]),
    ]
    for read in reads:
        read.start()
    for read, write in zip(reads, writes):
        read.wait()
        write.start()
    for write in writes:
        write.wait()


def shards(n_src, n_dst, raw, enc_w1, enc_w2, block_weights, block_cols, noise):
    blocks, side, _ = block_weights.shape
    hops, rows, width = noise.shape
    pairs = n_src // 2
    per_row = blocks // n_src
    part = width // CHUNKS
    assert rows == side and n_src % 2 == 0
    anywhere = pl.BlockSpec(memory_space=pl.ANY)
    dma = pltpu.SemaphoreType.DMA
    far = max(pairs - 1, 1)
    near = max(n_dst - 1, 1)
    encoded, kept = pl.pallas_call(
        functools.partial(kernel, n_src, n_dst, hops),
        out_shape=(
            jax.ShapeDtypeStruct((rows, width), BF16),
            jax.ShapeDtypeStruct((hops, rows, width), BF16),
        ),
        in_specs=[anywhere] * 4 + [pl.BlockSpec(memory_space=pltpu.SMEM), anywhere],
        out_specs=(anywhere, anywhere),
        scratch_shapes=[
            pltpu.VMEM(raw.shape, BF16),
            pltpu.VMEM(enc_w1.shape, BF16),
            pltpu.VMEM(enc_w2.shape, BF16),
            pltpu.VMEM(block_weights.shape, F32),
            pltpu.VMEM(noise.shape, BF16),
            pltpu.VMEM((rows, width), BF16),
            pltpu.VMEM((hops, rows, width), BF16),
            pltpu.VMEM((n_src, 2 * side, per_row * side), BF16),
            [[pltpu.VMEM((n_dst, rows, part), BF16) for _ in range(CHUNKS)] for _ in range(hops)],
            pltpu.VMEM((hops, CHUNKS, pairs, rows, part), BF16),
            pltpu.VMEM((hops, CHUNKS, pairs, rows, part), BF16),
            pltpu.VMEM((hops, CHUNKS, far, rows, part), BF16),
            pltpu.VMEM((hops, CHUNKS, far, rows, part), BF16),
            pltpu.VMEM((CHUNKS, rows, part), F32),
            dma((5,)),
            dma((hops + 1,)),
            dma((hops, CHUNKS, near)),
            dma((hops, CHUNKS, near)),
            dma((hops, CHUNKS, pairs)),
            dma((hops, CHUNKS, pairs)),
            dma((hops, CHUNKS, far)),
            dma((hops, CHUNKS, far)),
        ],
        compiler_params=pltpu.CompilerParams(
            collective_id=0, has_side_effects=True, vmem_limit_bytes=60 * 1024 * 1024
        ),
    )(raw, enc_w1, enc_w2, block_weights, block_cols, noise)
    shapes = (
        jax.ShapeDtypeStruct((rows, width), BF16),
        jax.ShapeDtypeStruct((hops, rows, width), BF16),
    )
    return pl.pallas_call(
        finish,
        out_shape=shapes,
        in_specs=[anywhere, anywhere],
        out_specs=(anywhere, anywhere),
        scratch_shapes=[pltpu.VMEM(s.shape, BF16) for s in shapes] + [dma((4,))],
    )(encoded, kept)


def solution(mesh):
    placed = (
        P(("src", "dst"), None),
        P(),
        P(),
        P(("src", "dst"), None, None),
        P(("src", "dst")),
        P(None, ("src", "dst"), None),
    )
    return jax.shard_map(
        functools.partial(shards, mesh.shape["src"], mesh.shape["dst"]),
        mesh=mesh,
        in_specs=placed,
        out_specs=(P(("src", "dst"), None), P(None, ("src", "dst"), None)),
        check_vma=False,
    )
```
